32 devices in a mesh: parts: 2 (over y), dp: 8 (over z, x), grad: 2 (over core).
Axes of the slice: x: 2, y: 2, z: 4, core: 2. Of those that a mesh axis runs over, the one named last changes fastest.
Arguments:
- activations: bfloat16 [32, 14, 14, 1024], P(('parts', 'dp', 'grad')), parts along dimension 0, may hold values from -12 to 12
- output_grads: bfloat16 [32, 14, 14, 1024], P(('parts', 'dp', 'grad')), parts along dimension 0, may hold values from -6 to 6
- owners: int32 [1024, 1], replicated, may hold values from 0 to 7; in each aligned block of 1024 rows (0 to 1023, 1024 to 2047, ...) at most 160 rows name the same one
Outputs:
- owned_inverse: float32 [2560, 2401], P(('parts', 'dp', 'grad')), parts along dimension 0
- update: float32 [49, 2048], P(None, 'parts'), parts along dimension 1
The draws below stay inside these ranges and needn't reach their ends.
There are 2 independent parts, one for each index of `parts`. The reference program is written for one: setup_inputs(seed, part) draws one part's arguments, and reference() takes and returns one part's arrays. A program takes and returns all parts, laid end to end along the dimension named above; an argument that names none is the same for every part. Nothing has to cross between parts.
Inputs may be any that keep to these rules, and one draw needn't show every extreme that they name: `owners`: no owner is named by more than 160 channels; some owner is named by exactly 160.
All inputs are finite; a program needn't handle non-finite values.
Results may differ from the reference program's by a relative error of at most 0.0003.
Values may be sent and summed in bfloat16 or wider, within the bound.
A program may use at most 128 MiB of HBM per device.

```python
import math
import jax
import jax.numpy as jnp
import numpy as np
from jax import lax

C = 1024
KS = 7
HW = 14
IMG_DEV = 1
TAPS = 49
NIMG = 16
POSITIONS = 3136
CAP = 160
SLOTS = 1280
N_DP = 8


def draw_activations(key, part):
    keys = jax.random.split(key, 5)
    shape = (NIMG, HW + 2, HW + 2, C)
    noise = jax.random.normal(keys[0], shape, jnp.float32)
    mixing = jax.random.uniform(keys[1], (3, 3, C), jnp.float32, 0.2, 1.0)
    norm_mix = jnp.sqrt(jnp.sum(mixing * mixing, axis=(0, 1)))
    smooth = jnp.zeros((NIMG, HW, HW, C), jnp.float32)
    for row_off in range(3):
        for col_off in range(3):
            smooth = smooth + mixing[row_off, col_off] * noise[:, row_off:row_off + HW, col_off:col_off + HW, :]
    smooth = smooth / norm_mix
    chan_scale = jnp.exp(jax.random.uniform(keys[2], (C,), jnp.float32, -0.7, 0.7))
    chan_mean = 0.5 * jax.random.normal(keys[3], (C,), jnp.float32)
    devices_n = NIMG // IMG_DEV
    chan_block = max(C // devices_n, 1)
    block_count = C // chan_block
    pairing = jax.random.permutation(keys[4], devices_n) % block_count
    image_dev = jnp.arange(NIMG, dtype=jnp.int32) // IMG_DEV
    chan_ids = jnp.arange(C, dtype=jnp.int32) // chan_block
    boost = 1.0 + 2.0 * (chan_ids[None, :] == pairing[image_dev][:, None]).astype(jnp.float32)
    values = (smooth * chan_scale + chan_mean) * boost[:, None, None, :]
    return jnp.clip(values, -12.0, 12.0).astype(jnp.bfloat16)


def raised(values, key, source, target, shards_of, factor):
    def block_of(axis_at):
        return (jnp.arange(values.shape[axis_at]) // (values.shape[axis_at] // shards_of)).reshape((-1,) + (1,) * (values.ndim - 1 - axis_at))

    near = jax.random.permutation(key, shards_of)[block_of(target)]
    second = (block_of(target) + shards_of // 2) % shards_of
    return jnp.where((block_of(source) == near) | (block_of(source) == second), factor * values, values)


def shard_levels(own_key, extent, cuts, low, high):
    loudness, own = 1.0, jax.random.fold_in(own_key, 6)
    for position, parts in cuts:
        steps = jnp.exp(jax.random.uniform(jax.random.fold_in(own, position), (parts,), jnp.float32, low / len(cuts), high / len(cuts)))
        loudness = loudness * jnp.repeat(steps, extent[position] // parts).reshape([-1 if axis == position else 1 for axis in range(len(extent))])
    return loudness


def assign_block(key, own, number, rows, count, top, reach, slope):
    ranking = jax.random.permutation(key, count)
    crowded, usual = portions_of(count, rows * top, reach, slope, True), portions_of(count, rows * top, reach, slope, False)
    places = jnp.arange(count)

    def named(tallies, turn):
        used = int((tallies > 0).sum())
        fixed = max(1, used // 4)
        shifted = fixed + (places - fixed + turn * (used - fixed)) % max(1, count - fixed)
        return jnp.zeros((count,), jnp.int32).at[ranking[jnp.where(places < fixed, places, shifted)]].set(jnp.asarray(tallies, jnp.int32))

    tallies = jnp.where(number % 4 == 0, named(crowded, number // 4), named(usual, number - number // 4 - 1))
    mixed = jax.random.permutation(jax.random.fold_in(own, 3), count)
    donor, receiver = mixed[0:count // 2 * 2:2], mixed[1:count // 2 * 2:2]
    room = jnp.minimum(tallies[donor] - 1, reach - tallies[receiver]) // 2
    room = jnp.where((donor == ranking[0]) | (receiver == ranking[0]) | (tallies[receiver] == 0), 0, jnp.maximum(room, 0))
    shifted = jax.random.randint(jax.random.fold_in(own, 4), (count // 2,), 0, 1 << 20) % (room + 1)
    tallies = tallies.at[donor].add(-shifted).at[receiver].add(shifted)
    labels = jnp.searchsorted(jnp.cumsum(tallies), jnp.arange(rows * top), side="right").astype(jnp.int32)
    grid = labels.reshape(top, rows).T
    grid = grid[jax.random.permutation(jax.random.fold_in(own, 1), rows)]
    turn = jax.random.randint(jax.random.fold_in(own, 2), (rows, 1), 0, top)
    return jnp.take_along_axis(grid, (jnp.arange(top)[None, :] + turn) % top, axis=1)


def portions_of(count, total, bound, skew, full):
    portions = [(1 << 20) // math.isqrt(grade ** skew) + 1 for grade in range(1, count + 1)]
    largest = bound if full else min(bound, max(-(-total // count), total * portions[0] // sum(portions)))
    least = 1 if total - largest >= count - 1 else 0
    holding, rest = [largest] + [least] * (count - 1), total - largest - least * (count - 1)
    while rest > 0:
        candidates = [i for i in range(1, count) if holding[i] < largest] or [i for i in range(1, count) if holding[i] < bound]
        pool, remaining = sum([portions[i] for i in candidates]), rest
        for i in candidates:
            addition = min(bound - holding[i], max(1, remaining * portions[i] // pool), rest)
            holding[i] = holding[i] + addition
            rest = rest - addition
    return np.array(holding)


def bell_draw_with(stream_key, extent, scale, reach, shards, heavy, kind=jnp.bfloat16):
    drawn = scale * jax.random.normal(stream_key, extent, jnp.float32)
    if shards:
        drawn = drawn * shard_levels(stream_key, extent, shards, -0.22, 0.18)
    return jnp.clip(raised(drawn, jax.random.fold_in(stream_key, 3), *heavy), -reach, reach).astype(kind)


def setup_inputs(seed: int = 0, part: int = 0) -> dict:
    arg_keys = jax.random.split(jax.random.key(seed), 4)
    part_keys = jax.random.split(jax.random.fold_in(arg_keys[3], part), 4)
    activations = draw_activations(jax.random.fold_in(jax.random.fold_in(arg_keys[3], part), 71), part)
    output_grads = bell_draw_with(part_keys[1], (NIMG, HW, HW, C), 1.0, 6.0, ((0, 16),), (0, 3, 16, 2.0))
    owners_keys = jax.random.split(jax.random.fold_in(arg_keys[2], 1), C // C)
    owners_turns = jax.random.permutation(jax.random.fold_in(arg_keys[2], 3), C // C)
    owners = jax.vmap(lambda own, number: assign_block(jax.random.fold_in(arg_keys[2], 2), own, number, C, N_DP, 1, CAP, 2))(owners_keys, owners_turns).reshape((C, 1))
    return dict(activations=activations, output_grads=output_grads, owners=owners)


def tap_stack(images):
    radius = (KS - 1) // 2
    padded = jnp.pad(images, ((0, 0), (radius, radius), (radius, radius), (0, 0)))
    width = images.shape[3]
    pieces = []
    for row_off in range(KS):
        for col_off in range(KS):
            pieces.append(padded[:, row_off:row_off + HW, col_off:col_off + HW, :].reshape(-1, width))
    return jnp.stack(pieces, axis=0)

def block_stats(pair):
    acts_blk, grads_blk = pair
    patches = tap_stack(acts_blk).astype(jnp.float32)
    grads_flat = grads_blk.reshape(-1, grads_blk.shape[3]).astype(jnp.float32)
    factor = jnp.einsum('tpc,spc->cts', patches, patches, precision=lax.Precision.HIGHEST)
    grad_sum = jnp.einsum('tpc,pc->ct', patches, grads_flat, precision=lax.Precision.HIGHEST)
    out_stat = lax.optimization_barrier(jnp.sum(grads_flat * grads_flat, axis=0))
    return (factor, grad_sum, out_stat)

def invert(factor):
    eye = jnp.eye(TAPS, dtype=jnp.float32)
    matrix = factor + 0.1 * eye
    lower = jnp.linalg.cholesky(matrix)
    lower_inv = jax.scipy.linalg.solve_triangular(lower, jnp.broadcast_to(eye, matrix.shape), lower=True)
    return jnp.einsum('kji,kjl->kil', lower_inv, lower_inv, precision=lax.Precision.HIGHEST)

def reference(activations, output_grads, owners):
    block = 32
    nblocks = C // block
    acts_b = jnp.moveaxis(activations.reshape(NIMG, HW, HW, nblocks, block), 3, 0)
    grads_b = jnp.moveaxis(output_grads.reshape(NIMG, HW, HW, nblocks, block), 3, 0)
    factor, grad_sum, out_stat = lax.map(block_stats, (acts_b, grads_b))
    factor = factor.reshape(C, TAPS, TAPS) / POSITIONS
    grad_sum = grad_sum.reshape(C, TAPS) / POSITIONS
    out_stat = out_stat.reshape(C) / POSITIONS
    owner_col = owners[:, 0]
    onehot = (owner_col[:, None] == jnp.arange(N_DP, dtype=jnp.int32)[None, :]).astype(jnp.int32)
    before = jnp.cumsum(onehot, axis=0) - onehot
    rank = lax.optimization_barrier(jnp.sum(before * onehot, axis=1)).astype(jnp.int32)
    slot = (owner_col * CAP + rank).astype(jnp.int32)
    inverse = invert(factor)
    owned_inverse = jnp.zeros((SLOTS, TAPS * TAPS), jnp.float32).at[slot].set(inverse.reshape(C, TAPS * TAPS))
    direction = jnp.einsum('kts,ks->kt', inverse, grad_sum, precision=lax.Precision.HIGHEST) / (out_stat[:, None] + 0.1)
    curvature = jnp.sum(direction * grad_sum)
    update = (direction * jnp.sqrt(TAPS * C / curvature)).T
    return (owned_inverse, update)
```

```python
import functools

import jax
import jax.numpy as jnp
from jax import lax
from jax.experimental import pallas as pl
from jax.experimental.pallas import tpu as pltpu
from jax.sharding import PartitionSpec as P

KS = 7
HW = 14
TAPS = 49
PIX = HW * HW
RAD = 3
LANES = 128
PADT = 56
ROWS = 2 * PIX + 8
F32 = jnp.float32
BF16 = jnp.bfloat16
VMEM_LIMIT = 60 * 1024 * 1024


def vmem_specs(count):
    return [pl.BlockSpec(memory_space=pltpu.VMEM)] * count


def route_kernel(slots_dev, capacity, act_ref, grad_ref, ocol_ref, orow_ref, out_ref, srow_ref,
                 data, scol):
    chans = act_ref.shape[1]
    step = pl.program_id(0)

    @pl.when(step == 0)
    def _():
        data[0:PIX, :] = act_ref[...]
        data[PIX:2 * PIX, :] = grad_ref[...]
        data[2 * PIX:ROWS, :] = jnp.ones((8, chans), BF16)
        ocol, orow = ocol_ref[...], orow_ref[...]
        sub = lax.broadcasted_iota(jnp.int32, (chans, chans), 0)
        lane = lax.broadcasted_iota(jnp.int32, (chans, chans), 1)
        same = ocol == orow
        rank_col = jnp.sum(jnp.where(same & (lane < sub), 1.0, 0.0), axis=1, keepdims=True)
        rank_row = jnp.sum(jnp.where(same & (sub < lane), 1.0, 0.0), axis=0, keepdims=True)
        scol[...] = ocol * capacity + rank_col.astype(jnp.int32)
        srow_ref[...] = orow * capacity + rank_row.astype(jnp.int32)

    lane = lax.broadcasted_iota(jnp.int32, (chans, 2 * LANES), 1)
    within = lane & (LANES - 1)
    target = jnp.where(
        within < slots_dev, (2 * step + (lane >> 7)) * slots_dev + within, -1
    )
    pick = jnp.where(scol[...] == target, 1.0, 0.0).astype(BF16)
    got = jnp.dot(data[...], pick, preferred_element_type=F32).astype(BF16)
    out_ref[0] = got[:, :LANES]
    out_ref[1] = got[:, LANES:]


def windows(parts, shift):
    size = abs(shift)
    edge = max(0, RAD - size)
    count = HW - size
    add = lambda items: functools.reduce(lambda p, q: p + q, items)
    mid = add(parts[edge:count - edge])
    if edge == 0:
        return [mid] * (KS - size)
    left, right = parts[:edge], parts[count - edge:]
    grow = [mid + add(left)]
    for item in right:
        grow.append(grow[-1] + item)
    shrink = [mid + add(right)]
    for item in left[:0:-1]:
        shrink.append(shrink[-1] + item)
    full = [grow[-1]] * (KS - size - 2 * edge)
    return grow[:edge] + full + shrink[::-1]


def owner_kernel(imgs, slots_dev, positions, recv_ref, inv_ref, dir_ref,
                 xs, gs, wide, narrow, mat, rowbuf, gbuf, gsum, flat):
    groups = imgs // 8
    scale = 1.0 / positions

    @pl.loop(0, imgs)
    def _(img):
        xs[pl.ds(img, PIX, stride=imgs), :] = recv_ref[img, 0:PIX, :].astype(F32)
        gs[pl.ds(img, PIX, stride=imgs), :] = recv_ref[img, PIX:2 * PIX, :].astype(F32)

    def pixel(ref, row, col, group):
        start = pl.multiple_of((row * HW + col) * imgs + 8 * group, 8)
        return ref[pl.ds(start, 8), :]

    zero = jnp.zeros((8, LANES), F32)

    def total(items):
        return functools.reduce(lambda p, q: p + q, items)

    @pl.loop(0, KS)
    def _(down):
        @pl.loop(0, HW - down)
        def _(row):
            for shift in range(-(KS - 1), KS):
                parts = []
                for col in range(max(0, -shift), HW - max(0, shift)):
                    parts.append(total([
                        pixel(xs, row, col, g) * pixel(xs, row + down, col + shift, g)
                        for g in range(groups)
                    ]))
                sums = windows(parts, shift)
                for place, value in enumerate(sums):
                    b = place + max(0, -shift)
                    start = pl.multiple_of(row * (PADT * 8), 8) + (b * 8 + b + shift) * 8
                    wide[pl.ds(start, 8), :] = value
            for b in range(KS):
                start = pl.multiple_of(row * (PADT * 8), 8) + (b * 8 + 7) * 8
                wide[pl.ds(start, 8), :] = zero

        @pl.loop(0, HW - down)
        def _(row):
            for b in range(KS):
                base = row * (PADT * 8) + b * 64
                value = total([wide[pl.ds(base + s, 8, stride=8), :] for s in range(8)])
                dst = pl.multiple_of((down * HW + row) * PADT, 8) + b * 8
                narrow[pl.ds(dst, 8), :] = value

    sub = lax.broadcasted_iota(jnp.int32, (8, LANES), 0)
    for a in range(KS):
        mat[a * 8 + 7] = jnp.zeros((PADT, LANES), F32)
    for b in range(KS):
        for down in range(KS):
            parts = [
                narrow[(down * HW + row) * PADT + b * 8:(down * HW + row) * PADT + b * 8 + 8, :]
                for row in range(HW - down)
            ]
            for a, value in enumerate(windows(parts, down)):
                value = value * scale
                if down == 0:
                    value = value + jnp.where(sub == b, 0.1, 0.0)
                mat[a * 8 + b, (a + down) * 8:(a + down) * 8 + 8, :] = value
    for a in range(KS):
        for a2 in range(a + 1, KS):
            for b2 in range(KS):
                cols = jnp.concatenate(
                    [mat[a * 8 + b, a2 * 8 + b2:a2 * 8 + b2 + 1, :] for b in range(8)], axis=0
                )
                mat[a2 * 8 + b2, a * 8:a * 8 + 8, :] = cols

    @pl.loop(0, KS)
    def _(a):
        def one(row, sums):
            out = []
            for b in range(KS):
                terms = [sums[b]]
                for col in range(max(0, RAD - b), min(HW, HW + RAD - b)):
                    for g in range(groups):
                        terms.append(
                            pixel(xs, row + a - RAD, col + b - RAD, g) * pixel(gs, row, col, g)
                        )
                out.append(total(terms))
            return tuple(out)

        sums = lax.fori_loop(
            jnp.maximum(0, RAD - a), jnp.minimum(HW, HW + RAD - a), one, (zero,) * KS
        )
        for b in range(KS):
            gbuf[b * 8:b * 8 + 8, :] = sums[b]
        gbuf[56:64, :] = zero
        value = total([gbuf[pl.ds(s, 8, stride=8), :] for s in range(8)])
        gsum[pl.ds(pl.multiple_of(a * 8, 8), 8), :] = value * scale

    def square(row, acc):
        for col in range(HW):
            for g in range(groups):
                value = pixel(gs, row, col, g)
                acc = acc + value * value
        return acc

    stat = jnp.sum(lax.fori_loop(0, HW, square, zero), axis=0, keepdims=True) * scale

    subs = lax.broadcasted_iota(jnp.int32, (PADT, LANES), 0)
    for a in range(KS):
        @pl.loop(0, KS)
        def _(b):
            k = a * 8 + b
            row = mat[k]
            rowbuf[0:PADT, :] = row
            inv = 1.0 / rowbuf[pl.ds(k, 1), :]
            swept = jnp.where(subs == k, -inv, row * inv)
            at_pivot = sub == b
            for i in [p * 8 + q for p in range(KS) for q in range(KS)]:
                coef = jnp.broadcast_to(rowbuf[i:i + 1, :], (8, LANES))
                for tile in range(KS):
                    old = mat[i, tile * 8:tile * 8 + 8, :]
                    if tile == a:
                        old = jnp.where(at_pivot, 0.0, old)
                    mat[i, tile * 8:tile * 8 + 8, :] = old - coef * swept[tile * 8:tile * 8 + 8, :]
            mat[k] = swept

    valid = recv_ref[0, 2 * PIX:ROWS, :].astype(F32)
    acc = jnp.zeros((PADT, LANES), F32)
    for a in range(KS):
        for b in range(KS):
            i = a * 8 + b
            row = mat[i]
            acc = acc - gsum[i:i + 1, :] * row
            for tile in range(KS):
                start = (a * KS + b) * TAPS + tile * KS
                flat[start:start + 8, :] = -row[tile * 8:tile * 8 + 8, :] * valid
    direction = acc / (stat + 0.1)
    product = jnp.sum(direction * gsum[...], axis=0, keepdims=True)
    dir_ref[...] = direction
    dir_ref[7:8, :] = product
    for start in range(0, TAPS * TAPS, LANES):
        width = min(LANES, TAPS * TAPS - start)
        block = jnp.transpose(flat[start:start + LANES, :])
        inv_ref[:, start:start + width] = block[:slots_dev, :width]


def update_kernel(devices_n, slots_dev, chans, dirs_ref, srow_ref, out_ref, acc):
    acc[...] = jnp.zeros_like(acc)
    lane_slot = lax.broadcasted_iota(jnp.int32, (LANES, chans), 0)

    def one(dev, curv):
        value = dirs_ref[dev]
        wanted = srow_ref[...] - dev * slots_dev
        pick = jnp.where((lane_slot == wanted) & (lane_slot < slots_dev), 1.0, 0.0).astype(BF16)
        high = value.astype(BF16)
        rest = value - high.astype(F32)
        mid = rest.astype(BF16)
        low = (rest - mid.astype(F32)).astype(BF16)
        for piece in (high, mid, low):
            acc[...] += jnp.dot(piece, pick, preferred_element_type=F32)
        return curv + value[0:8, :]

    sums = lax.fori_loop(0, devices_n, one, jnp.zeros((8, LANES), F32))
    curvature = jnp.sum(sums[7:8, :], axis=1, keepdims=True)
    factor = jnp.sqrt(TAPS * chans / curvature)
    for a in range(KS):
        out_ref[a * KS:a * KS + KS, :] = acc[a * 8:a * 8 + KS, :] * factor


def route(act, grad, owners, devices_n, slots_dev, capacity):
    chans = act.shape[1]
    whole = lambda *shape: pl.BlockSpec(shape, lambda d: (0,) * len(shape))
    return pl.pallas_call(
        functools.partial(route_kernel, slots_dev, capacity),
        grid=(devices_n // 2,),
        in_specs=[whole(PIX, chans), whole(PIX, chans), whole(chans, 1), whole(1, chans)],
        out_specs=[pl.BlockSpec((2, ROWS, LANES), lambda d: (d, 0, 0)), whole(1, chans)],
        out_shape=[
            jax.ShapeDtypeStruct((devices_n, ROWS, LANES), BF16),
            jax.ShapeDtypeStruct((1, chans), jnp.int32),
        ],
        scratch_shapes=[pltpu.VMEM((ROWS, chans), BF16), pltpu.VMEM((chans, 1), jnp.int32)],
        compiler_params=pltpu.CompilerParams(vmem_limit_bytes=VMEM_LIMIT),
        name="route",
    )(act, grad, owners, owners.reshape(1, chans))


def own(recv, slots_dev, positions):
    imgs = recv.shape[0]
    return pl.pallas_call(
        functools.partial(owner_kernel, imgs, slots_dev, positions),
        in_specs=vmem_specs(1),
        out_specs=vmem_specs(2),
        out_shape=[
            jax.ShapeDtypeStruct((slots_dev, TAPS * TAPS), F32),
            jax.ShapeDtypeStruct((PADT, LANES), F32),
        ],
        scratch_shapes=[
            pltpu.VMEM((PIX * imgs, LANES), F32),
            pltpu.VMEM((PIX * imgs, LANES), F32),
            pltpu.VMEM((HW * PADT * 8, LANES), F32),
            pltpu.VMEM((KS * HW * PADT, LANES), F32),
            pltpu.VMEM((PADT, PADT, LANES), F32),
            pltpu.VMEM((64, LANES), F32),
            pltpu.VMEM((64, LANES), F32),
            pltpu.VMEM((PADT, LANES), F32),
            pltpu.VMEM((19 * LANES, LANES), F32),
        ],
        compiler_params=pltpu.CompilerParams(vmem_limit_bytes=VMEM_LIMIT),
        name="own",
    )(recv)


def spread(dirs, srow, slots_dev):
    devices_n, chans = dirs.shape[0], srow.shape[1]
    return pl.pallas_call(
        functools.partial(update_kernel, devices_n, slots_dev, chans),
        in_specs=vmem_specs(2),
        out_specs=pl.BlockSpec(memory_space=pltpu.VMEM),
        out_shape=jax.ShapeDtypeStruct((TAPS, chans), F32),
        scratch_shapes=[pltpu.VMEM((PADT, chans), F32)],
        compiler_params=pltpu.CompilerParams(vmem_limit_bytes=VMEM_LIMIT),
        name="spread",
    )(dirs, srow)


def per_device(activations, output_grads, owners):
    devices_n = lax.axis_size(("dp", "grad"))
    owners_n = lax.axis_size("dp")
    chans = activations.shape[3]
    capacity = 5 * chans // (4 * owners_n)
    slots_dev = owners_n * capacity // devices_n
    positions = PIX * devices_n
    send, srow = route(
        activations.reshape(PIX, chans), output_grads.reshape(PIX, chans), owners,
        devices_n, slots_dev, capacity,
    )
    recv = lax.all_to_all(send, ("dp", "grad"), 0, 0, tiled=True)
    owned_inverse, direction = own(recv, slots_dev, positions)
    dirs = lax.all_gather(direction, ("dp", "grad"), axis=0, tiled=False)
    return owned_inverse, spread(dirs, srow, slots_dev)


def solution(mesh):
    in_specs = (
        P(("parts", "dp", "grad"), None, None, None),
        P(("parts", "dp", "grad"), None, None, None),
        P(),
    )
    out_specs = (P(("parts", "dp", "grad"), None), P(None, "parts"))
    return jax.shard_map(
        per_device, mesh=mesh, in_specs=in_specs, out_specs=out_specs, check_vma=False
    )
```

```python
import functools

import jax
import jax.numpy as jnp
from jax import lax
from jax.experimental import pallas as pl
from jax.experimental.pallas import tpu as pltpu
from jax.sharding import PartitionSpec as P

KS = 7
HW = 14
TAPS = 49
PIX = HW * HW
RAD = 3
LANES = 128
PADT = 56
PIXP = 200
USED = 80
MESH = pl.DeviceIdType.MESH
F32 = jnp.float32
BF16 = jnp.bfloat16
VMEM_LIMIT = 60 * 1024 * 1024


def vmem_specs(count):
    return [pl.BlockSpec(memory_space=pltpu.VMEM)] * count


def peer_at(index):
    cores = lax.axis_size("grad")
    return {"dp": lax.div(index, cores), "grad": lax.rem(index, cores)}


def greet(devices_n, me):
    barrier = pltpu.get_barrier_semaphore()

    @pl.loop(1, devices_n)
    def _(off):
        pl.semaphore_signal(
            barrier, inc=1, device_id=peer_at(lax.rem(me + off, devices_n)), device_id_type=MESH
        )

    return barrier


def pack(value, lane):
    one = jnp.where(lane[:72] >= USED, pltpu.roll(value[128:200], 80, 1), value[0:72])
    two = jnp.where(lane[:56] >= USED, pltpu.roll(value[128:184], 32, 1), value[72:128])
    far = lane[:16] >= 112
    return jnp.concatenate([
        one,
        jnp.where(far, pltpu.roll(value[184:200], 64, 1), two[0:16]),
        jnp.where(far, pltpu.roll(value[184:200], 48, 1), two[16:32]),
        two[32:56],
    ], axis=0)


def unpack(value, lane):
    head = jnp.where(lane < USED, value, 0.0)
    low = lane[:72] < 48
    first = pltpu.roll(value[0:72], 48, 1)
    rest = jnp.concatenate([
        pltpu.roll(value[72:128], 96, 1),
        jnp.where(
            lane[:16] < 64,
            pltpu.roll(value[72:88], 64, 1),
            pltpu.roll(value[88:104], 80, 1),
        ),
    ], axis=0)
    tail = jnp.where(low, first, jnp.where(lane[:72] < USED, rest, 0.0))
    return head, tail


def exchange_kernel(devices_n, owners_n, slots_dev, capacity, act_ref, grad_ref, orow_ref,
                    recv_ref, srow_ref, stage, data, send, send_sem, recv_sem, self_sem):
    chans = act_ref.shape[2]
    me = lax.axis_index(("dp", "grad"))
    barrier = greet(devices_n, me)
    for i in range(HW):
        stage[i * HW:i * HW + HW, :] = act_ref[i].astype(F32)
        stage[200 + i * HW:200 + i * HW + HW, :] = grad_ref[i].astype(F32)
    ones = jnp.ones((4, chans), F32)
    stage[PIX:200, :] = ones
    stage[200 + PIX:400, :] = ones
    data[...] = stage[...].astype(BF16)
    orow = orow_ref[...]
    mine = lax.broadcasted_iota(jnp.int32, (owners_n, chans), 0) == orow
    before = jnp.where(
        lax.broadcasted_iota(jnp.int32, (chans, chans), 0)
        < lax.broadcasted_iota(jnp.int32, (chans, chans), 1), 1.0, 0.0
    ).astype(BF16)
    earlier = jnp.dot(jnp.where(mine, 1.0, 0.0).astype(BF16), before, preferred_element_type=F32)
    rank = jnp.sum(jnp.where(mine, earlier, 0.0), axis=0, keepdims=True)
    slot = orow * capacity + rank.astype(jnp.int32)
    srow_ref[...] = slot
    lane = lax.broadcasted_iota(jnp.int32, (128, LANES), 1)
    sub = lax.broadcasted_iota(jnp.int32, (2 * LANES, chans), 0)
    within = sub & (LANES - 1)
    offset = jnp.where(within < slots_dev, (sub >> 7) * slots_dev + within, -chans * 8)

    def fill(pair):
        pick = jnp.where(srow_ref[...] - 2 * pair * slots_dev == offset, 1.0, 0.0).astype(BF16)
        got = lax.dot_general(
            data[...], pick, (((1,), (1,)), ((), ())), preferred_element_type=F32
        )
        for core in range(2):
            cols = got[:, core * LANES:(core + 1) * LANES]
            send[2 * pair + core, 0:128] = pack(cols[0:200], lane).astype(BF16)
            send[2 * pair + core, 128:256] = pack(cols[200:400], lane).astype(BF16)

    def copy_to(dev):
        return pltpu.make_async_remote_copy(
            src_ref=send.at[dev], dst_ref=recv_ref.at[me],
            send_sem=send_sem.at[dev], recv_sem=recv_sem.at[me],
            device_id=peer_at(dev), device_id_type=MESH,
        )

    def copy_from(dev):
        return pltpu.make_async_remote_copy(
            src_ref=send.at[dev], dst_ref=recv_ref.at[dev],
            send_sem=send_sem.at[dev], recv_sem=recv_sem.at[dev],
            device_id=peer_at(dev), device_id_type=MESH,
        )

    pairs = devices_n // 2
    my_pair = lax.div(me, 2)
    pl.semaphore_wait(barrier, devices_n - 1)

    @pl.loop(1, pairs)
    def _(off):
        pair = lax.rem(my_pair + off, pairs)
        fill(pair)
        copy_to(2 * pair).start()
        copy_to(2 * pair + 1).start()

    fill(my_pair)
    copy_to(4 * my_pair + 1 - me).start()
    own_copy = pltpu.make_async_copy(send.at[me], recv_ref.at[me], self_sem)
    own_copy.start()

    @pl.loop(1, devices_n)
    def _(off):
        dev = lax.rem(me + off, devices_n)
        copy_from(dev).wait_send()
        copy_from(dev).wait_recv()

    own_copy.wait()


def gather_kernel(devices_n, dir_ref, out_ref, send_sem, recv_sem, self_sem):
    me = lax.axis_index(("dp", "grad"))
    barrier = greet(devices_n, me)

    def copy(dev, block):
        return pltpu.make_async_remote_copy(
            src_ref=dir_ref, dst_ref=out_ref.at[block],
            send_sem=send_sem.at[dev], recv_sem=recv_sem.at[block],
            device_id=peer_at(dev), device_id_type=MESH,
        )

    own_copy = pltpu.make_async_copy(dir_ref, out_ref.at[me], self_sem)
    own_copy.start()
    pl.semaphore_wait(barrier, devices_n - 1)

    @pl.loop(1, devices_n)
    def _(off):
        copy(lax.rem(me + off, devices_n), me).start()

    @pl.loop(1, devices_n)
    def _(off):
        dev = lax.rem(me + off, devices_n)
        copy(dev, dev).wait_send()
        copy(dev, dev).wait_recv()

    own_copy.wait()


def windows(parts, shift):
    size = abs(shift)
    edge = max(0, RAD - size)
    count = HW - size
    add = lambda items: functools.reduce(lambda p, q: p + q, items)
    mid = add(parts[edge:count - edge])
    if edge == 0:
        return [mid] * (KS - size)
    left, right = parts[:edge], parts[count - edge:]
    grow = [mid + add(left)]
    for item in right:
        grow.append(grow[-1] + item)
    shrink = [mid + add(right)]
    for item in left[:0:-1]:
        shrink.append(shrink[-1] + item)
    full = [grow[-1]] * (KS - size - 2 * edge)
    return grow[:edge] + full + shrink[::-1]


def owner_kernel(imgs, slots_dev, positions, recv_ref, inv_ref, dir_ref,
                 xs, gs, wide, narrow, mat, rowbuf, gbuf, gsum, flat):
    groups = imgs // 8
    scale = 1.0 / positions

    lane = lax.broadcasted_iota(jnp.int32, (128, LANES), 1)

    @pl.loop(0, imgs)
    def _(img):
        for ref, start in ((xs, 0), (gs, 128)):
            head, tail = unpack(recv_ref[img, start:start + 128, :].astype(F32), lane)
            ref[pl.ds(img, 128, stride=imgs), :] = head
            ref[pl.ds(128 * imgs + img, 72, stride=imgs), :] = tail

    def pixel(ref, row, col, group):
        start = pl.multiple_of((row * HW + col) * imgs + 8 * group, 8)
        return ref[pl.ds(start, 8), :]

    zero = jnp.zeros((8, LANES), F32)

    def total(items):
        return functools.reduce(lambda p, q: p + q, items)

    @pl.loop(0, KS)
    def _(down):
        @pl.loop(0, HW - down)
        def _(row):
            for shift in range(-(KS - 1), KS):
                parts = []
                for col in range(max(0, -shift), HW - max(0, shift)):
                    parts.append(total([
                        pixel(xs, row, col, g) * pixel(xs, row + down, col + shift, g)
                        for g in range(groups)
                    ]))
                sums = windows(parts, shift)
                for place, value in enumerate(sums):
                    b = place + max(0, -shift)
                    start = pl.multiple_of(row * (PADT * 8), 8) + (b * 8 + b + shift) * 8
                    wide[pl.ds(start, 8), :] = value
            for b in range(KS):
                start = pl.multiple_of(row * (PADT * 8), 8) + (b * 8 + 7) * 8
                wide[pl.ds(start, 8), :] = zero

        @pl.loop(0, HW - down)
        def _(row):
            for b in range(KS):
                base = row * (PADT * 8) + b * 64
                value = total([wide[pl.ds(base + s, 8, stride=8), :] for s in range(8)])
                dst = pl.multiple_of((down * HW + row) * PADT, 8) + b * 8
                narrow[pl.ds(dst, 8), :] = value

    sub = lax.broadcasted_iota(jnp.int32, (8, LANES), 0)
    for a in range(KS):
        mat[a * 8 + 7] = jnp.zeros((PADT, LANES), F32)
    for b in range(KS):
        for down in range(KS):
            parts = [
                narrow[(down * HW + row) * PADT + b * 8:(down * HW + row) * PADT + b * 8 + 8, :]
                for row in range(HW - down)
            ]
            for a, value in enumerate(windows(parts, down)):
                value = value * scale
                if down == 0:
                    value = value + jnp.where(sub == b, 0.1, 0.0)
                mat[a * 8 + b, (a + down) * 8:(a + down) * 8 + 8, :] = value
    for a in range(KS):
        for a2 in range(a + 1, KS):
            for b2 in range(KS):
                cols = jnp.concatenate(
                    [mat[a * 8 + b, a2 * 8 + b2:a2 * 8 + b2 + 1, :] for b in range(8)], axis=0
                )
                mat[a2 * 8 + b2, a * 8:a * 8 + 8, :] = cols

    @pl.loop(0, KS)
    def _(a):
        def one(row, sums):
            out = []
            for b in range(KS):
                terms = [sums[b]]
                for col in range(max(0, RAD - b), min(HW, HW + RAD - b)):
                    for g in range(groups):
                        terms.append(
                            pixel(xs, row + a - RAD, col + b - RAD, g) * pixel(gs, row, col, g)
                        )
                out.append(total(terms))
            return tuple(out)

        sums = lax.fori_loop(
            jnp.maximum(0, RAD - a), jnp.minimum(HW, HW + RAD - a), one, (zero,) * KS
        )
        for b in range(KS):
            gbuf[b * 8:b * 8 + 8, :] = sums[b]
        gbuf[56:64, :] = zero
        value = total([gbuf[pl.ds(s, 8, stride=8), :] for s in range(8)])
        gsum[pl.ds(pl.multiple_of(a * 8, 8), 8), :] = value * scale

    def square(row, acc):
        for col in range(HW):
            for g in range(groups):
                value = pixel(gs, row, col, g)
                acc = acc + value * value
        return acc

    stat = jnp.sum(lax.fori_loop(0, HW, square, zero), axis=0, keepdims=True) * scale

    subs = lax.broadcasted_iota(jnp.int32, (PADT, LANES), 0)
    for a in range(KS):
        @pl.loop(0, KS)
        def _(b):
            k = a * 8 + b
            row = mat[k]
            rowbuf[0:PADT, :] = row
            inv = 1.0 / rowbuf[pl.ds(k, 1), :]
            swept = jnp.where(subs == k, -inv, row * inv)
            at_pivot = sub == b
            for i in [p * 8 + q for p in range(KS) for q in range(KS)]:
                coef = jnp.broadcast_to(rowbuf[i:i + 1, :], (8, LANES))
                for tile in range(KS):
                    old = mat[i, tile * 8:tile * 8 + 8, :]
                    if tile == a:
                        old = jnp.where(at_pivot, 0.0, old)
                    mat[i, tile * 8:tile * 8 + 8, :] = old - coef * swept[tile * 8:tile * 8 + 8, :]
            mat[k] = swept

    valid = jnp.broadcast_to(xs[PIX * imgs:PIX * imgs + 1, :], (8, LANES))
    acc = jnp.zeros((PADT, LANES), F32)
    for a in range(KS):
        for b in range(KS):
            i = a * 8 + b
            row = mat[i]
            acc = acc - gsum[i:i + 1, :] * row
            for tile in range(KS):
                start = (a * KS + b) * TAPS + tile * KS
                flat[start:start + 8, :] = -row[tile * 8:tile * 8 + 8, :] * valid
    direction = acc / (stat + 0.1)
    product = jnp.sum(direction * gsum[...], axis=0, keepdims=True)
    dir_ref[...] = direction
    dir_ref[7:8, :] = product
    for start in range(0, TAPS * TAPS, LANES):
        width = min(LANES, TAPS * TAPS - start)
        block = jnp.transpose(flat[start:start + LANES, :])
        inv_ref[:, start:start + width] = block[:slots_dev, :width]


def update_kernel(devices_n, slots_dev, chans, dirs_ref, srow_ref, out_ref, acc):
    acc[...] = jnp.zeros_like(acc)
    lane_slot = lax.broadcasted_iota(jnp.int32, (LANES, chans), 0)

    def one(dev, curv):
        value = dirs_ref[dev]
        wanted = srow_ref[...] - dev * slots_dev
        pick = jnp.where((lane_slot == wanted) & (lane_slot < slots_dev), 1.0, 0.0).astype(BF16)
        high = value.astype(BF16)
        rest = value - high.astype(F32)
        mid = rest.astype(BF16)
        low = (rest - mid.astype(F32)).astype(BF16)
        for piece in (high, mid, low):
            acc[...] += jnp.dot(piece, pick, preferred_element_type=F32)
        return curv + value[0:8, :]

    sums = lax.fori_loop(0, devices_n, one, jnp.zeros((8, LANES), F32))
    curvature = jnp.sum(sums[7:8, :], axis=1, keepdims=True)
    factor = jnp.sqrt(TAPS * chans / curvature)
    for a in range(KS):
        out_ref[a * KS:a * KS + KS, :] = acc[a * 8:a * 8 + KS, :] * factor


def exchange(act, grad, owners, devices_n, owners_n, slots_dev, capacity):
    chans = act.shape[2]
    return pl.pallas_call(
        functools.partial(exchange_kernel, devices_n, owners_n, slots_dev, capacity),
        in_specs=vmem_specs(3),
        out_specs=[pl.BlockSpec(memory_space=pl.ANY), pl.BlockSpec(memory_space=pltpu.VMEM)],
        out_shape=[
            jax.ShapeDtypeStruct((devices_n, 256, LANES), BF16),
            jax.ShapeDtypeStruct((1, chans), jnp.int32),
        ],
        scratch_shapes=[
            pltpu.VMEM((2 * PIXP, chans), F32),
            pltpu.VMEM((2 * PIXP, chans), BF16),
            pltpu.VMEM((devices_n, 256, LANES), BF16),
            pltpu.SemaphoreType.DMA((devices_n,)),
            pltpu.SemaphoreType.DMA((devices_n,)),
            pltpu.SemaphoreType.DMA,
        ],
        compiler_params=pltpu.CompilerParams(
            collective_id=0, has_side_effects=True, vmem_limit_bytes=VMEM_LIMIT
        ),
        name="exchange",
    )(act, grad, owners.reshape(1, chans))


def gather(direction, devices_n):
    return pl.pallas_call(
        functools.partial(gather_kernel, devices_n),
        in_specs=vmem_specs(1),
        out_specs=pl.BlockSpec(memory_space=pltpu.VMEM),
        out_shape=jax.ShapeDtypeStruct((devices_n,) + direction.shape, F32),
        scratch_shapes=[
            pltpu.SemaphoreType.DMA((devices_n,)),
            pltpu.SemaphoreType.DMA((devices_n,)),
            pltpu.SemaphoreType.DMA,
        ],
        compiler_params=pltpu.CompilerParams(collective_id=1, has_side_effects=True),
        name="gather",
    )(direction)


def own(recv, slots_dev, positions):
    imgs = recv.shape[0]
    return pl.pallas_call(
        functools.partial(owner_kernel, imgs, slots_dev, positions),
        in_specs=vmem_specs(1),
        out_specs=vmem_specs(2),
        out_shape=[
            jax.ShapeDtypeStruct((slots_dev, TAPS * TAPS), F32),
            jax.ShapeDtypeStruct((PADT, LANES), F32),
        ],
        scratch_shapes=[
            pltpu.VMEM((PIXP * imgs, LANES), F32),
            pltpu.VMEM((PIXP * imgs, LANES), F32),
            pltpu.VMEM((HW * PADT * 8, LANES), F32),
            pltpu.VMEM((KS * HW * PADT, LANES), F32),
            pltpu.VMEM((PADT, PADT, LANES), F32),
            pltpu.VMEM((64, LANES), F32),
            pltpu.VMEM((64, LANES), F32),
            pltpu.VMEM((PADT, LANES), F32),
            pltpu.VMEM((19 * LANES, LANES), F32),
        ],
        compiler_params=pltpu.CompilerParams(vmem_limit_bytes=VMEM_LIMIT),
        name="own",
    )(recv)


def spread(dirs, srow, slots_dev):
    devices_n, chans = dirs.shape[0], srow.shape[1]
    return pl.pallas_call(
        functools.partial(update_kernel, devices_n, slots_dev, chans),
        in_specs=vmem_specs(2),
        out_specs=pl.BlockSpec(memory_space=pltpu.VMEM),
        out_shape=jax.ShapeDtypeStruct((TAPS, chans), F32),
        scratch_shapes=[pltpu.VMEM((PADT, chans), F32)],
        compiler_params=pltpu.CompilerParams(vmem_limit_bytes=VMEM_LIMIT),
        name="spread",
    )(dirs, srow)


def per_device(activations, output_grads, owners):
    devices_n = lax.axis_size(("dp", "grad"))
    owners_n = lax.axis_size("dp")
    chans = activations.shape[3]
    capacity = 5 * chans // (4 * owners_n)
    slots_dev = owners_n * capacity // devices_n
    positions = PIX * devices_n
    recv, srow = exchange(
        activations[0], output_grads[0], owners, devices_n, owners_n, slots_dev, capacity
    )
    owned_inverse, direction = own(recv, slots_dev, positions)
    dirs = gather(direction, devices_n)
    return owned_inverse, spread(dirs, srow, slots_dev)


def solution(mesh):
    in_specs = (
        P(("parts", "dp", "grad"), None, None, None),
        P(("parts", "dp", "grad"), None, None, None),
        P(),
    )
    out_specs = (P(("parts", "dp", "grad"), None), P(None, "parts"))
    return jax.shard_map(
        per_device, mesh=mesh, in_specs=in_specs, out_specs=out_specs, check_vma=False
    )
```

```python
import functools

import jax
import jax.numpy as jnp
from jax import lax
from jax.experimental import pallas as pl
from jax.experimental.pallas import tpu as pltpu
from jax.sharding import PartitionSpec as P

KS = 7
HW = 14
TAPS = 49
PIX = HW * HW
RAD = 3
LANES = 128
PADT = 56
PIXP = 200
USED = 80
MESH = pl.DeviceIdType.MESH
F32 = jnp.float32
BF16 = jnp.bfloat16
VMEM_LIMIT = 60 * 1024 * 1024


def vmem_specs(count):
    return [pl.BlockSpec(memory_space=pltpu.VMEM)] * count


def peer_at(index):
    cores = lax.axis_size("grad")
    return {"dp": lax.div(index, cores), "grad": lax.rem(index, cores)}


def greet(devices_n, me):
    barrier = pltpu.get_barrier_semaphore()

    @pl.loop(1, devices_n)
    def _(off):
        pl.semaphore_signal(
            barrier, inc=1, device_id=peer_at(lax.rem(me + off, devices_n)), device_id_type=MESH
        )

    return barrier


def pack(value, lane):
    one = jnp.where(lane[:72] >= USED, pltpu.roll(value[128:200], 80, 1), value[0:72])
    two = jnp.where(lane[:56] >= USED, pltpu.roll(value[128:184], 32, 1), value[72:128])
    far = lane[:16] >= 112
    return jnp.concatenate([
        one,
        jnp.where(far, pltpu.roll(value[184:200], 64, 1), two[0:16]),
        jnp.where(far, pltpu.roll(value[184:200], 48, 1), two[16:32]),
        two[32:56],
    ], axis=0)


def unpack(value, lane):
    head = jnp.where(lane < USED, value, 0.0)
    low = lane[:72] < 48
    first = pltpu.roll(value[0:72], 48, 1)
    rest = jnp.concatenate([
        pltpu.roll(value[72:128], 96, 1),
        jnp.where(
            lane[:16] < 64,
            pltpu.roll(value[72:88], 64, 1),
            pltpu.roll(value[88:104], 80, 1),
        ),
    ], axis=0)
    tail = jnp.where(low, first, jnp.where(lane[:72] < USED, rest, 0.0))
    return head, tail


def exchange_kernel(devices_n, owners_n, slots_dev, capacity, act_ref, grad_ref, orow_ref,
                    recv_ref, srow_ref, stage, data, send, send_sem, recv_sem, self_sem):
    chans = act_ref.shape[2]
    me = lax.axis_index(("dp", "grad"))
    barrier = greet(devices_n, me)
    for i in range(HW):
        stage[i * HW:i * HW + HW, :] = act_ref[i].astype(F32)
        stage[200 + i * HW:200 + i * HW + HW, :] = grad_ref[i].astype(F32)
    ones = jnp.ones((4, chans), F32)
    stage[PIX:200, :] = ones
    stage[200 + PIX:400, :] = ones
    data[...] = stage[...].astype(BF16)
    orow = orow_ref[...]
    mine = lax.broadcasted_iota(jnp.int32, (owners_n, chans), 0) == orow
    before = jnp.where(
        lax.broadcasted_iota(jnp.int32, (chans, chans), 0)
        < lax.broadcasted_iota(jnp.int32, (chans, chans), 1), 1.0, 0.0
    ).astype(BF16)
    earlier = jnp.dot(jnp.where(mine, 1.0, 0.0).astype(BF16), before, preferred_element_type=F32)
    rank = jnp.sum(jnp.where(mine, earlier, 0.0), axis=0, keepdims=True)
    slot = orow * capacity + rank.astype(jnp.int32)
    srow_ref[...] = slot
    lane = lax.broadcasted_iota(jnp.int32, (128, LANES), 1)
    sub = lax.broadcasted_iota(jnp.int32, (2 * LANES, chans), 0)
    within = sub & (LANES - 1)
    offset = jnp.where(within < slots_dev, (sub >> 7) * slots_dev + within, -chans * 8)

    def fill(pair):
        pick = jnp.where(srow_ref[...] - 2 * pair * slots_dev == offset, 1.0, 0.0).astype(BF16)
        got = lax.dot_general(
            data[...], pick, (((1,), (1,)), ((), ())), preferred_element_type=F32
        )
        for core in range(2):
            cols = got[:, core * LANES:(core + 1) * LANES]
            send[2 * pair + core, 0:128] = pack(cols[0:200], lane).astype(BF16)
            send[2 * pair + core, 128:256] = pack(cols[200:400], lane).astype(BF16)

    def copy_to(dev):
        return pltpu.make_async_remote_copy(
            src_ref=send.at[dev], dst_ref=recv_ref.at[me],
            send_sem=send_sem.at[dev], recv_sem=recv_sem.at[me],
            device_id=peer_at(dev), device_id_type=MESH,
        )

    def copy_from(dev):
        return pltpu.make_async_remote_copy(
            src_ref=send.at[dev], dst_ref=recv_ref.at[dev],
            send_sem=send_sem.at[dev], recv_sem=recv_sem.at[dev],
            device_id=peer_at(dev), device_id_type=MESH,
        )

    pairs = devices_n // 2
    my_pair = lax.div(me, 2)
    pl.semaphore_wait(barrier, devices_n - 1)

    @pl.loop(0, pairs - 1)
    def _(turn):
        side = 2 * lax.rem(turn, 2) - 1
        off = pairs // 2 + side * lax.div(turn + 1, 2)
        pair = lax.rem(my_pair + off, pairs)
        fill(pair)
        copy_to(2 * pair).start()
        copy_to(2 * pair + 1).start()

    fill(my_pair)
    copy_to(4 * my_pair + 1 - me).start()
    own_copy = pltpu.make_async_copy(send.at[me], recv_ref.at[me], self_sem)
    own_copy.start()

    @pl.loop(1, devices_n)
    def _(off):
        dev = lax.rem(me + off, devices_n)
        copy_from(dev).wait_send()
        copy_from(dev).wait_recv()

    own_copy.wait()


def gather_kernel(devices_n, slots_dev, chans, dir_ref, srow_ref, out_ref,
                  dirs, acc, send_sem, recv_sem, pass_sem):
    me = lax.axis_index(("dp", "grad"))
    pairs = devices_n // 2
    my_pair = lax.div(me, 2)
    core = me - 2 * my_pair
    sibling = 2 * my_pair + 1 - core
    barrier = greet(devices_n, me)

    def near(off):
        return 2 * lax.rem(my_pair + off, pairs) + core

    def far(off):
        return 2 * lax.rem(my_pair + off, pairs) + 1 - core

    def direct(dev, block):
        return pltpu.make_async_remote_copy(
            src_ref=dir_ref, dst_ref=dirs.at[block],
            send_sem=send_sem.at[dev], recv_sem=recv_sem.at[block],
            device_id=peer_at(dev), device_id_type=MESH,
        )

    def passed(block, landing):
        return pltpu.make_async_remote_copy(
            src_ref=dirs.at[block], dst_ref=dirs.at[landing],
            send_sem=pass_sem.at[block], recv_sem=recv_sem.at[landing],
            device_id=peer_at(sibling), device_id_type=MESH,
        )

    lane_slot = lax.broadcasted_iota(jnp.int32, (LANES, chans), 0)
    lane_slot = jnp.where(lane_slot < slots_dev, lane_slot, -8 * chans)

    def place(dev, value):
        pick = jnp.where(lane_slot == srow_ref[...] - dev * slots_dev, 1.0, 0.0).astype(BF16)
        high = value.astype(BF16)
        rest = value - high.astype(F32)
        mid = rest.astype(BF16)
        low = (rest - mid.astype(F32)).astype(BF16)
        return (
            jnp.dot(high, pick, preferred_element_type=F32)
            + jnp.dot(mid, pick, preferred_element_type=F32)
            + jnp.dot(low, pick, preferred_element_type=F32)
        )

    pl.semaphore_wait(barrier, devices_n - 1)

    @pl.loop(1, pairs)
    def _(off):
        direct(near(off), me).start()

    direct(sibling, me).start()
    acc[...] = place(me, dir_ref[...])

    def take_near(off, curv):
        dev = near(off)
        direct(dev, dev).wait_recv()
        passed(dev, dev).start()
        value = dirs[dev]
        acc[...] += place(dev, value)
        return curv + value[0:8, :]

    curv = lax.fori_loop(1, pairs, take_near, dir_ref[0:8, :])

    def take_far(off, curv):
        dev = far(off)
        passed(dev, dev).wait_recv()
        value = dirs[dev]
        acc[...] += place(dev, value)
        return curv + value[0:8, :]

    curv = lax.fori_loop(0, pairs, take_far, curv)

    @pl.loop(1, pairs)
    def _(off):
        dev = near(off)
        direct(dev, dev).wait_send()
        passed(dev, dev).wait_send()

    direct(sibling, sibling).wait_send()
    curvature = jnp.sum(curv[7:8, :], axis=1, keepdims=True)
    factor = jnp.sqrt(TAPS * chans / curvature)
    for a in range(KS):
        out_ref[a * KS:a * KS + KS, :] = acc[a * 8:a * 8 + KS, :] * factor


def windows(parts, shift):
    size = abs(shift)
    edge = max(0, RAD - size)
    count = HW - size
    add = lambda items: functools.reduce(lambda p, q: p + q, items)
    mid = add(parts[edge:count - edge])
    if edge == 0:
        return [mid] * (KS - size)
    left, right = parts[:edge], parts[count - edge:]
    grow = [mid + add(left)]
    for item in right:
        grow.append(grow[-1] + item)
    shrink = [mid + add(right)]
    for item in left[:0:-1]:
        shrink.append(shrink[-1] + item)
    full = [grow[-1]] * (KS - size - 2 * edge)
    return grow[:edge] + full + shrink[::-1]


def owner_kernel(imgs, slots_dev, positions, recv_ref, inv_ref, dir_ref,
                 xs, gs, wide, narrow, mat, rowbuf, gbuf, gsum, flat):
    groups = imgs // 8
    scale = 1.0 / positions

    lane = lax.broadcasted_iota(jnp.int32, (128, LANES), 1)

    @pl.loop(0, imgs)
    def _(img):
        for ref, start in ((xs, 0), (gs, 128)):
            head, tail = unpack(recv_ref[img, start:start + 128, :].astype(F32), lane)
            ref[pl.ds(img, 128, stride=imgs), :] = head
            ref[pl.ds(128 * imgs + img, 72, stride=imgs), :] = tail

    def pixel(ref, row, col, group):
        start = pl.multiple_of((row * HW + col) * imgs + 8 * group, 8)
        return ref[pl.ds(start, 8), :]

    zero = jnp.zeros((8, LANES), F32)

    def total(items):
        return functools.reduce(lambda p, q: p + q, items)

    @pl.loop(0, KS)
    def _(down):
        @pl.loop(0, HW - down)
        def _(row):
            for shift in range(-(KS - 1), KS):
                parts = []
                for col in range(max(0, -shift), HW - max(0, shift)):
                    parts.append(total([
                        pixel(xs, row, col, g) * pixel(xs, row + down, col + shift, g)
                        for g in range(groups)
                    ]))
                sums = windows(parts, shift)
                for place, value in enumerate(sums):
                    b = place + max(0, -shift)
                    start = pl.multiple_of(row * (PADT * 8), 8) + (b * 8 + b + shift) * 8
                    wide[pl.ds(start, 8), :] = value
            for b in range(KS):
                start = pl.multiple_of(row * (PADT * 8), 8) + (b * 8 + 7) * 8
                wide[pl.ds(start, 8), :] = zero

        @pl.loop(0, HW - down)
        def _(row):
            for b in range(KS):
                base = row * (PADT * 8) + b * 64
                value = total([wide[pl.ds(base + s, 8, stride=8), :] for s in range(8)])
                dst = pl.multiple_of((down * HW + row) * PADT, 8) + b * 8
                narrow[pl.ds(dst, 8), :] = value

    sub = lax.broadcasted_iota(jnp.int32, (8, LANES), 0)
    for a in range(KS):
        mat[a * 8 + 7] = jnp.zeros((PADT, LANES), F32)
    for b in range(KS):
        for down in range(KS):
            parts = [
                narrow[(down * HW + row) * PADT + b * 8:(down * HW + row) * PADT + b * 8 + 8, :]
                for row in range(HW - down)
            ]
            for a, value in enumerate(windows(parts, down)):
                value = value * scale
                if down == 0:
                    value = value + jnp.where(sub == b, 0.1, 0.0)
                mat[a * 8 + b, (a + down) * 8:(a + down) * 8 + 8, :] = value
    for a in range(KS):
        for a2 in range(a + 1, KS):
            for b2 in range(KS):
                cols = jnp.concatenate(
                    [mat[a * 8 + b, a2 * 8 + b2:a2 * 8 + b2 + 1, :] for b in range(8)], axis=0
                )
                mat[a2 * 8 + b2, a * 8:a * 8 + 8, :] = cols

    @pl.loop(0, KS)
    def _(a):
        def one(row, sums):
            out = []
            for b in range(KS):
                terms = [sums[b]]
                for col in range(max(0, RAD - b), min(HW, HW + RAD - b)):
                    for g in range(groups):
                        terms.append(
                            pixel(xs, row + a - RAD, col + b - RAD, g) * pixel(gs, row, col, g)
                        )
                out.append(total(terms))
            return tuple(out)

        sums = lax.fori_loop(
            jnp.maximum(0, RAD - a), jnp.minimum(HW, HW + RAD - a), one, (zero,) * KS
        )
        for b in range(KS):
            gbuf[b * 8:b * 8 + 8, :] = sums[b]
        gbuf[56:64, :] = zero
        value = total([gbuf[pl.ds(s, 8, stride=8), :] for s in range(8)])
        gsum[pl.ds(pl.multiple_of(a * 8, 8), 8), :] = value * scale

    def square(row, acc):
        for col in range(HW):
            for g in range(groups):
                value = pixel(gs, row, col, g)
                acc = acc + value * value
        return acc

    stat = jnp.sum(lax.fori_loop(0, HW, square, zero), axis=0, keepdims=True) * scale

    subs = lax.broadcasted_iota(jnp.int32, (PADT, LANES), 0)
    for a in range(KS):
        @pl.loop(0, KS)
        def _(b):
            k = a * 8 + b
            row = mat[k]
            rowbuf[0:PADT, :] = row
            inv = 1.0 / rowbuf[pl.ds(k, 1), :]
            swept = jnp.where(subs == k, -inv, row * inv)
            at_pivot = sub == b
            for i in [p * 8 + q for p in range(KS) for q in range(KS)]:
                coef = jnp.broadcast_to(rowbuf[i:i + 1, :], (8, LANES))
                for tile in range(KS):
                    old = mat[i, tile * 8:tile * 8 + 8, :]
                    if tile == a:
                        old = jnp.where(at_pivot, 0.0, old)
                    mat[i, tile * 8:tile * 8 + 8, :] = old - coef * swept[tile * 8:tile * 8 + 8, :]
            mat[k] = swept

    valid = jnp.broadcast_to(xs[PIX * imgs:PIX * imgs + 1, :], (8, LANES))
    acc = jnp.zeros((PADT, LANES), F32)
    for a in range(KS):
        for b in range(KS):
            i = a * 8 + b
            row = mat[i]
            acc = acc - gsum[i:i + 1, :] * row
            for tile in range(KS):
                start = (a * KS + b) * TAPS + tile * KS
                flat[start:start + 8, :] = -row[tile * 8:tile * 8 + 8, :] * valid
    direction = acc / (stat + 0.1)
    product = jnp.sum(direction * gsum[...], axis=0, keepdims=True)
    dir_ref[...] = direction
    dir_ref[7:8, :] = product
    for start in range(0, TAPS * TAPS, LANES):
        width = min(LANES, TAPS * TAPS - start)
        block = jnp.transpose(flat[start:start + LANES, :])
        inv_ref[:, start:start + width] = block[:slots_dev, :width]


def exchange(act, grad, owners, devices_n, owners_n, slots_dev, capacity):
    chans = act.shape[2]
    return pl.pallas_call(
        functools.partial(exchange_kernel, devices_n, owners_n, slots_dev, capacity),
        in_specs=vmem_specs(3),
        out_specs=[pl.BlockSpec(memory_space=pl.ANY), pl.BlockSpec(memory_space=pltpu.VMEM)],
        out_shape=[
            jax.ShapeDtypeStruct((devices_n, 256, LANES), BF16),
            jax.ShapeDtypeStruct((1, chans), jnp.int32),
        ],
        scratch_shapes=[
            pltpu.VMEM((2 * PIXP, chans), F32),
            pltpu.VMEM((2 * PIXP, chans), BF16),
            pltpu.VMEM((devices_n, 256, LANES), BF16),
            pltpu.SemaphoreType.DMA((devices_n,)),
            pltpu.SemaphoreType.DMA((devices_n,)),
            pltpu.SemaphoreType.DMA,
        ],
        compiler_params=pltpu.CompilerParams(
            collective_id=0, has_side_effects=True, vmem_limit_bytes=VMEM_LIMIT
        ),
        name="exchange",
    )(act, grad, owners.reshape(1, chans))


def gather(direction, srow, devices_n, slots_dev):
    chans = srow.shape[1]
    return pl.pallas_call(
        functools.partial(gather_kernel, devices_n, slots_dev, chans),
        in_specs=vmem_specs(2),
        out_specs=pl.BlockSpec(memory_space=pltpu.VMEM),
        out_shape=jax.ShapeDtypeStruct((TAPS, chans), F32),
        scratch_shapes=[
            pltpu.VMEM((devices_n, PADT, LANES), F32),
            pltpu.VMEM((PADT, chans), F32),
            pltpu.SemaphoreType.DMA((devices_n,)),
            pltpu.SemaphoreType.DMA((devices_n,)),
            pltpu.SemaphoreType.DMA((devices_n,)),
        ],
        compiler_params=pltpu.CompilerParams(
            collective_id=1, has_side_effects=True, vmem_limit_bytes=VMEM_LIMIT
        ),
        name="gather",
    )(direction, srow)


def own(recv, slots_dev, positions):
    imgs = recv.shape[0]
    return pl.pallas_call(
        functools.partial(owner_kernel, imgs, slots_dev, positions),
        in_specs=vmem_specs(1),
        out_specs=vmem_specs(2),
        out_shape=[
            jax.ShapeDtypeStruct((slots_dev, TAPS * TAPS), F32),
            jax.ShapeDtypeStruct((PADT, LANES), F32),
        ],
        scratch_shapes=[
            pltpu.VMEM((PIXP * imgs, LANES), F32),
            pltpu.VMEM((PIXP * imgs, LANES), F32),
            pltpu.VMEM((HW * PADT * 8, LANES), F32),
            pltpu.VMEM((KS * HW * PADT, LANES), F32),
            pltpu.VMEM((PADT, PADT, LANES), F32),
            pltpu.VMEM((64, LANES), F32),
            pltpu.VMEM((64, LANES), F32),
            pltpu.VMEM((PADT, LANES), F32),
            pltpu.VMEM((19 * LANES, LANES), F32),
        ],
        compiler_params=pltpu.CompilerParams(vmem_limit_bytes=VMEM_LIMIT),
        name="own",
    )(recv)


def per_device(activations, output_grads, owners):
    devices_n = lax.axis_size(("dp", "grad"))
    owners_n = lax.axis_size("dp")
    chans = activations.shape[3]
    capacity = 5 * chans // (4 * owners_n)
    slots_dev = owners_n * capacity // devices_n
    positions = PIX * devices_n
    recv, srow = exchange(
        activations[0], output_grads[0], owners, devices_n, owners_n, slots_dev, capacity
    )
    owned_inverse, direction = own(recv, slots_dev, positions)
    return owned_inverse, gather(direction, srow, devices_n, slots_dev)


def solution(mesh):
    in_specs = (
        P(("parts", "dp", "grad"), None, None, None),
        P(("parts", "dp", "grad"), None, None, None),
        P(),
    )
    out_specs = (P(("parts", "dp", "grad"), None), P(None, "parts"))
    return jax.shard_map(
        per_device, mesh=mesh, in_specs=in_specs, out_specs=out_specs, check_vma=False
    )
```

```python
import functools

import jax
import jax.numpy as jnp
from jax import lax
from jax.experimental import pallas as pl
from jax.experimental.pallas import tpu as pltpu
from jax.sharding import PartitionSpec as P

KS = 7
HW = 14
TAPS = 49
PIX = HW * HW
RAD = 3
LANES = 128
PADT = 56
PIXP = 200
USED = 80
MESH = pl.DeviceIdType.MESH
F32 = jnp.float32
BF16 = jnp.bfloat16
VMEM_LIMIT = 60 * 1024 * 1024


def vmem_specs(count):
    return [pl.BlockSpec(memory_space=pltpu.VMEM)] * count


def peer_at(index):
    cores = lax.axis_size("grad")
    return {"dp": lax.div(index, cores), "grad": lax.rem(index, cores)}


def greet(devices_n, me):
    barrier = pltpu.get_barrier_semaphore()

    @pl.loop(1, devices_n)
    def _(off):
        pl.semaphore_signal(
            barrier, inc=1, device_id=peer_at(lax.rem(me + off, devices_n)), device_id_type=MESH
        )

    return barrier


def pack(value, lane):
    one = jnp.where(lane[:72] >= USED, pltpu.roll(value[128:200], 80, 1), value[0:72])
    two = jnp.where(lane[:56] >= USED, pltpu.roll(value[128:184], 32, 1), value[72:128])
    far = lane[:16] >= 112
    return jnp.concatenate([
        one,
        jnp.where(far, pltpu.roll(value[184:200], 64, 1), two[0:16]),
        jnp.where(far, pltpu.roll(value[184:200], 48, 1), two[16:32]),
        two[32:56],
    ], axis=0)


def unpack(value, lane):
    head = jnp.where(lane < USED, value, 0.0)
    low = lane[:72] < 48
    first = pltpu.roll(value[0:72], 48, 1)
    rest = jnp.concatenate([
        pltpu.roll(value[72:128], 96, 1),
        jnp.where(
            lane[:16] < 64,
            pltpu.roll(value[72:88], 64, 1),
            pltpu.roll(value[88:104], 80, 1),
        ),
    ], axis=0)
    tail = jnp.where(low, first, jnp.where(lane[:72] < USED, rest, 0.0))
    return head, tail


def exchange_kernel(devices_n, owners_n, slots_dev, capacity, act_ref, grad_ref, orow_ref,
                    recv_ref, srow_ref, stage, data, send, send_sem, recv_sem, self_sem):
    chans = act_ref.shape[2]
    me = lax.axis_index(("dp", "grad"))
    barrier = greet(devices_n, me)
    for i in range(HW):
        stage[i * HW:i * HW + HW, :] = act_ref[i].astype(F32)
        stage[200 + i * HW:200 + i * HW + HW, :] = grad_ref[i].astype(F32)
    ones = jnp.ones((4, chans), F32)
    stage[PIX:200, :] = ones
    stage[200 + PIX:400, :] = ones
    data[...] = stage[...].astype(BF16)
    orow = orow_ref[...]
    mine = lax.broadcasted_iota(jnp.int32, (owners_n, chans), 0) == orow
    before = jnp.where(
        lax.broadcasted_iota(jnp.int32, (chans, chans), 0)
        < lax.broadcasted_iota(jnp.int32, (chans, chans), 1), 1.0, 0.0
    ).astype(BF16)
    earlier = jnp.dot(jnp.where(mine, 1.0, 0.0).astype(BF16), before, preferred_element_type=F32)
    rank = jnp.sum(jnp.where(mine, earlier, 0.0), axis=0, keepdims=True)
    slot = orow * capacity + rank.astype(jnp.int32)
    srow_ref[...] = slot
    lane = lax.broadcasted_iota(jnp.int32, (128, LANES), 1)
    sub = lax.broadcasted_iota(jnp.int32, (2 * LANES, chans), 0)
    within = sub & (LANES - 1)
    offset = jnp.where(within < slots_dev, (sub >> 7) * slots_dev + within, -chans * 8)

    def fill(pair):
        pick = jnp.where(srow_ref[...] - 2 * pair * slots_dev == offset, 1.0, 0.0).astype(BF16)
        got = lax.dot_general(
            data[...], pick, (((1,), (1,)), ((), ())), preferred_element_type=F32
        )
        for core in range(2):
            cols = got[:, core * LANES:(core + 1) * LANES]
            send[2 * pair + core, 0:128] = pack(cols[0:200], lane).astype(BF16)
            send[2 * pair + core, 128:256] = pack(cols[200:400], lane).astype(BF16)

    def copy_to(dev):
        return pltpu.make_async_remote_copy(
            src_ref=send.at[dev], dst_ref=recv_ref.at[me],
            send_sem=send_sem.at[dev], recv_sem=recv_sem.at[me],
            device_id=peer_at(dev), device_id_type=MESH,
        )

    def copy_from(dev):
        return pltpu.make_async_remote_copy(
            src_ref=send.at[dev], dst_ref=recv_ref.at[dev],
            send_sem=send_sem.at[dev], recv_sem=recv_sem.at[dev],
            device_id=peer_at(dev), device_id_type=MESH,
        )

    pairs = devices_n // 2
    my_pair = lax.div(me, 2)
    pl.semaphore_wait(barrier, devices_n - 1)

    @pl.loop(0, pairs - 1)
    def _(turn):
        side = 2 * lax.rem(turn, 2) - 1
        off = pairs // 2 + side * lax.div(turn + 1, 2)
        pair = lax.rem(my_pair + off, pairs)
        fill(pair)
        copy_to(2 * pair).start()
        copy_to(2 * pair + 1).start()

    fill(my_pair)
    copy_to(4 * my_pair + 1 - me).start()
    own_copy = pltpu.make_async_copy(send.at[me], recv_ref.at[me], self_sem)
    own_copy.start()

    @pl.loop(1, devices_n)
    def _(off):
        dev = lax.rem(me + off, devices_n)
        copy_from(dev).wait_send()
        copy_from(dev).wait_recv()

    own_copy.wait()


def gather_kernel(devices_n, slots_dev, chans, dir_ref, srow_ref, out_ref,
                  dirs, acc, send_sem, recv_sem, pass_sem):
    me = lax.axis_index(("dp", "grad"))
    pairs = devices_n // 2
    my_pair = lax.div(me, 2)
    core = me - 2 * my_pair
    sibling = 2 * my_pair + 1 - core
    barrier = greet(devices_n, me)

    def near(off):
        return 2 * lax.rem(my_pair + off, pairs) + core

    def far(off):
        return 2 * lax.rem(my_pair + off, pairs) + 1 - core

    def direct(dev, block):
        return pltpu.make_async_remote_copy(
            src_ref=dir_ref, dst_ref=dirs.at[block],
            send_sem=send_sem.at[dev], recv_sem=recv_sem.at[block],
            device_id=peer_at(dev), device_id_type=MESH,
        )

    def passed(block, landing):
        return pltpu.make_async_remote_copy(
            src_ref=dirs.at[block], dst_ref=dirs.at[landing],
            send_sem=pass_sem.at[block], recv_sem=recv_sem.at[landing],
            device_id=peer_at(sibling), device_id_type=MESH,
        )

    lane_slot = lax.broadcasted_iota(jnp.int32, (LANES, chans), 0)
    lane_slot = jnp.where(lane_slot < slots_dev, lane_slot, -8 * chans)

    def place(dev, value):
        pick = jnp.where(lane_slot == srow_ref[...] - dev * slots_dev, 1.0, 0.0).astype(BF16)
        high = value.astype(BF16)
        rest = value - high.astype(F32)
        mid = rest.astype(BF16)
        low = (rest - mid.astype(F32)).astype(BF16)
        return (
            jnp.dot(high, pick, preferred_element_type=F32)
            + jnp.dot(mid, pick, preferred_element_type=F32)
            + jnp.dot(low, pick, preferred_element_type=F32)
        )

    pl.semaphore_wait(barrier, devices_n - 1)

    @pl.loop(1, pairs)
    def _(off):
        direct(near(off), me).start()

    direct(sibling, me).start()
    acc[...] = place(me, dir_ref[...])

    def take_near(off, curv):
        dev = near(off)
        direct(dev, dev).wait_recv()
        passed(dev, dev).start()
        value = dirs[dev]
        acc[...] += place(dev, value)
        return curv + value[0:8, :]

    curv = lax.fori_loop(1, pairs, take_near, dir_ref[0:8, :])

    def take_far(off, curv):
        dev = far(off)
        passed(dev, dev).wait_recv()
        value = dirs[dev]
        acc[...] += place(dev, value)
        return curv + value[0:8, :]

    curv = lax.fori_loop(0, pairs, take_far, curv)

    @pl.loop(1, pairs)
    def _(off):
        dev = near(off)
        direct(dev, dev).wait_send()
        passed(dev, dev).wait_send()

    direct(sibling, sibling).wait_send()
    curvature = jnp.sum(curv[7:8, :], axis=1, keepdims=True)
    factor = jnp.sqrt(TAPS * chans / curvature)
    for a in range(KS):
        out_ref[a * KS:a * KS + KS, :] = acc[a * 8:a * 8 + KS, :] * factor


def windows(parts, shift):
    size = abs(shift)
    edge = max(0, RAD - size)
    count = HW - size
    add = lambda items: functools.reduce(lambda p, q: p + q, items)
    mid = add(parts[edge:count - edge])
    if edge == 0:
        return [mid] * (KS - size)
    left, right = parts[:edge], parts[count - edge:]
    grow = [mid + add(left)]
    for item in right:
        grow.append(grow[-1] + item)
    shrink = [mid + add(right)]
    for item in left[:0:-1]:
        shrink.append(shrink[-1] + item)
    full = [grow[-1]] * (KS - size - 2 * edge)
    return grow[:edge] + full + shrink[::-1]


def owner_kernel(imgs, slots_dev, positions, recv_ref, inv_ref, dir_ref,
                 xs, gs, wide, narrow, mat, rowbuf, gbuf, gsum, flat):
    groups = imgs // 8
    scale = 1.0 / positions

    lane = lax.broadcasted_iota(jnp.int32, (128, LANES), 1)

    @pl.loop(0, imgs)
    def _(img):
        for ref, start in ((xs, 0), (gs, 128)):
            head, tail = unpack(recv_ref[img, start:start + 128, :].astype(F32), lane)
            ref[pl.ds(img, 128, stride=imgs), :] = head
            ref[pl.ds(128 * imgs + img, 72, stride=imgs), :] = tail

    def pixel(ref, row, col, group):
        start = pl.multiple_of((row * HW + col) * imgs + 8 * group, 8)
        return ref[pl.ds(start, 8), :]

    zero = jnp.zeros((8, LANES), F32)

    def total(items):
        return functools.reduce(lambda p, q: p + q, items)

    @pl.loop(0, KS)
    def _(down):
        @pl.loop(0, HW - down)
        def _(row):
            here = [[pixel(xs, row, col, g) for g in range(groups)] for col in range(HW)]
            for shift in range(-(KS - 1), KS):
                parts = []
                for col in range(max(0, -shift), HW - max(0, shift)):
                    parts.append(total([
                        here[col][g] * pixel(xs, row + down, col + shift, g)
                        for g in range(groups)
                    ]))
                sums = windows(parts, shift)
                for place, value in enumerate(sums):
                    b = place + max(0, -shift)
                    start = pl.multiple_of(row * (PADT * 8), 8) + (b * 8 + b + shift) * 8
                    wide[pl.ds(start, 8), :] = value
            for b in range(KS):
                start = pl.multiple_of(row * (PADT * 8), 8) + (b * 8 + 7) * 8
                wide[pl.ds(start, 8), :] = zero

        @pl.loop(0, HW - down)
        def _(row):
            for b in range(KS):
                base = row * (PADT * 8) + b * 64
                value = total([wide[pl.ds(base + s, 8, stride=8), :] for s in range(8)])
                dst = pl.multiple_of((down * HW + row) * PADT, 8) + b * 8
                narrow[pl.ds(dst, 8), :] = value

    sub = lax.broadcasted_iota(jnp.int32, (8, LANES), 0)
    for a in range(KS):
        mat[a * 8 + 7] = jnp.zeros((PADT, LANES), F32)
    for b in range(KS):
        for down in range(KS):
            parts = [
                narrow[(down * HW + row) * PADT + b * 8:(down * HW + row) * PADT + b * 8 + 8, :]
                for row in range(HW - down)
            ]
            for a, value in enumerate(windows(parts, down)):
                value = value * scale
                if down == 0:
                    value = value + jnp.where(sub == b, 0.1, 0.0)
                mat[a * 8 + b, (a + down) * 8:(a + down) * 8 + 8, :] = value
    for a in range(KS):
        for a2 in range(a + 1, KS):
            for b2 in range(KS):
                cols = jnp.concatenate(
                    [mat[a * 8 + b, a2 * 8 + b2:a2 * 8 + b2 + 1, :] for b in range(8)], axis=0
                )
                mat[a2 * 8 + b2, a * 8:a * 8 + 8, :] = cols

    @pl.loop(0, KS)
    def _(a):
        def one(row, sums):
            out = []
            here = [[pixel(gs, row, col, g) for g in range(groups)] for col in range(HW)]
            for b in range(KS):
                terms = [sums[b]]
                for col in range(max(0, RAD - b), min(HW, HW + RAD - b)):
                    for g in range(groups):
                        terms.append(
                            pixel(xs, row + a - RAD, col + b - RAD, g) * here[col][g]
                        )
                out.append(total(terms))
            return tuple(out)

        sums = lax.fori_loop(
            jnp.maximum(0, RAD - a), jnp.minimum(HW, HW + RAD - a), one, (zero,) * KS
        )
        for b in range(KS):
            gbuf[b * 8:b * 8 + 8, :] = sums[b]
        gbuf[56:64, :] = zero
        value = total([gbuf[pl.ds(s, 8, stride=8), :] for s in range(8)])
        gsum[pl.ds(pl.multiple_of(a * 8, 8), 8), :] = value * scale

    def square(row, acc):
        for col in range(HW):
            for g in range(groups):
                value = pixel(gs, row, col, g)
                acc = acc + value * value
        return acc

    stat = jnp.sum(lax.fori_loop(0, HW, square, zero), axis=0, keepdims=True) * scale

    subs = lax.broadcasted_iota(jnp.int32, (PADT, LANES), 0)
    for a in range(KS):
        @pl.loop(0, KS)
        def _(b):
            k = a * 8 + b
            row = mat[k]
            rowbuf[0:PADT, :] = row
            inv = 1.0 / rowbuf[pl.ds(k, 1), :]
            swept = jnp.where(subs == k, -inv, row * inv)
            at_pivot = sub == b
            for i in [p * 8 + q for p in range(KS) for q in range(KS)]:
                coef = jnp.broadcast_to(rowbuf[i:i + 1, :], (8, LANES))
                for tile in range(KS):
                    old = mat[i, tile * 8:tile * 8 + 8, :]
                    if tile == a:
                        old = jnp.where(at_pivot, 0.0, old)
                    mat[i, tile * 8:tile * 8 + 8, :] = old - coef * swept[tile * 8:tile * 8 + 8, :]
            mat[k] = swept

    valid = jnp.broadcast_to(xs[PIX * imgs:PIX * imgs + 1, :], (8, LANES))
    acc = jnp.zeros((PADT, LANES), F32)
    for a in range(KS):
        for b in range(KS):
            i = a * 8 + b
            row = mat[i]
            acc = acc - gsum[i:i + 1, :] * row
            for tile in range(KS):
                start = (a * KS + b) * TAPS + tile * KS
                flat[start:start + 8, :] = -row[tile * 8:tile * 8 + 8, :] * valid
    direction = acc / (stat + 0.1)
    product = jnp.sum(direction * gsum[...], axis=0, keepdims=True)
    dir_ref[...] = direction
    dir_ref[7:8, :] = product
    for start in range(0, TAPS * TAPS, LANES):
        width = min(LANES, TAPS * TAPS - start)
        block = jnp.transpose(flat[start:start + LANES, :])
        inv_ref[:, start:start + width] = block[:slots_dev, :width]


def exchange(act, grad, owners, devices_n, owners_n, slots_dev, capacity):
    chans = act.shape[2]
    return pl.pallas_call(
        functools.partial(exchange_kernel, devices_n, owners_n, slots_dev, capacity),
        in_specs=vmem_specs(3),
        out_specs=[pl.BlockSpec(memory_space=pl.ANY), pl.BlockSpec(memory_space=pltpu.VMEM)],
        out_shape=[
            jax.ShapeDtypeStruct((devices_n, 256, LANES), BF16),
            jax.ShapeDtypeStruct((1, chans), jnp.int32),
        ],
        scratch_shapes=[
            pltpu.VMEM((2 * PIXP, chans), F32),
            pltpu.VMEM((2 * PIXP, chans), BF16),
            pltpu.VMEM((devices_n, 256, LANES), BF16),
            pltpu.SemaphoreType.DMA((devices_n,)),
            pltpu.SemaphoreType.DMA((devices_n,)),
            pltpu.SemaphoreType.DMA,
        ],
        compiler_params=pltpu.CompilerParams(
            collective_id=0, has_side_effects=True, vmem_limit_bytes=VMEM_LIMIT
        ),
        name="exchange",
    )(act, grad, owners.reshape(1, chans))


def gather(direction, srow, devices_n, slots_dev):
    chans = srow.shape[1]
    return pl.pallas_call(
        functools.partial(gather_kernel, devices_n, slots_dev, chans),
        in_specs=vmem_specs(2),
        out_specs=pl.BlockSpec(memory_space=pltpu.VMEM),
        out_shape=jax.ShapeDtypeStruct((TAPS, chans), F32),
        scratch_shapes=[
            pltpu.VMEM((devices_n, PADT, LANES), F32),
            pltpu.VMEM((PADT, chans), F32),
            pltpu.SemaphoreType.DMA((devices_n,)),
            pltpu.SemaphoreType.DMA((devices_n,)),
            pltpu.SemaphoreType.DMA((devices_n,)),
        ],
        compiler_params=pltpu.CompilerParams(
            collective_id=1, has_side_effects=True, vmem_limit_bytes=VMEM_LIMIT
        ),
        name="gather",
    )(direction, srow)


def own(recv, slots_dev, positions):
    imgs = recv.shape[0]
    return pl.pallas_call(
        functools.partial(owner_kernel, imgs, slots_dev, positions),
        in_specs=vmem_specs(1),
        out_specs=vmem_specs(2),
        out_shape=[
            jax.ShapeDtypeStruct((slots_dev, TAPS * TAPS), F32),
            jax.ShapeDtypeStruct((PADT, LANES), F32),
        ],
        scratch_shapes=[
            pltpu.VMEM((PIXP * imgs, LANES), F32),
            pltpu.VMEM((PIXP * imgs, LANES), F32),
            pltpu.VMEM((HW * PADT * 8, LANES), F32),
            pltpu.VMEM((KS * HW * PADT, LANES), F32),
            pltpu.VMEM((PADT, PADT, LANES), F32),
            pltpu.VMEM((64, LANES), F32),
            pltpu.VMEM((64, LANES), F32),
            pltpu.VMEM((PADT, LANES), F32),
            pltpu.VMEM((19 * LANES, LANES), F32),
        ],
        compiler_params=pltpu.CompilerParams(vmem_limit_bytes=VMEM_LIMIT),
        name="own",
    )(recv)


def per_device(activations, output_grads, owners):
    devices_n = lax.axis_size(("dp", "grad"))
    owners_n = lax.axis_size("dp")
    chans = activations.shape[3]
    capacity = 5 * chans // (4 * owners_n)
    slots_dev = owners_n * capacity // devices_n
    positions = PIX * devices_n
    recv, srow = exchange(
        activations[0], output_grads[0], owners, devices_n, owners_n, slots_dev, capacity
    )
    owned_inverse, direction = own(recv, slots_dev, positions)
    return owned_inverse, gather(direction, srow, devices_n, slots_dev)


def solution(mesh):
    in_specs = (
        P(("parts", "dp", "grad"), None, None, None),
        P(("parts", "dp", "grad"), None, None, None),
        P(),
    )
    out_specs = (P(("parts", "dp", "grad"), None), P(None, "parts"))
    return jax.shard_map(
        per_device, mesh=mesh, in_specs=in_specs, out_specs=out_specs, check_vma=False
    )
```
